128 devices in a mesh: gx: 8 (over x, core), gy: 16 (over y, z).
Axes of the slice: x: 4, y: 4, z: 4, core: 2. Of those that a mesh axis runs over, the one named last changes fastest.
Arguments:
- features: bfloat16 [8, 16, 2, 96, 4096], P('gx', 'gy'), may hold values from -6 to 6
- grad_out: bfloat16 [8, 16, 2, 96, 4096], P('gx', 'gy'), may hold values from -6 to 6
- weight: bfloat16 [96, 2592], replicated, may hold values from -0.125 to 0.125
- active: int32 [8, 16, 2], P('gx', 'gy'), may hold values from 0 to 1, as said below
Outputs:
- out: bfloat16 [8, 16, 2, 96, 4096], P('gx', 'gy')
- grad_in: bfloat16 [8, 16, 2, 96, 4096], P('gx', 'gy')
- grad_weight: float32 [248832], P(('gx', 'gy'))
The draws below stay inside these ranges and needn't reach their ends.
Inputs may be any that keep to these rules, and one draw needn't show every extreme that they name: The two columns with the same gx index and gy indices 2m and 2m + 1 hold exactly 2 active bricks together, so a column holds 0 to 2 of them; some column holds 2 in every draw.
All inputs are finite; a program needn't handle non-finite values.
Results may differ from the reference program's by a relative error of at most 0.001.
Values may be sent and summed in bfloat16 or wider, within the bound.
No kernel may reach another device: no remote copies, remote signals or barrier semaphores. Data moves between devices by JAX's collectives and lax.ppermute only.
A program may use at most 128 MiB of HBM per device.

```python
import math
import jax
import jax.numpy as jnp
from jax import lax

C = 96
EDGE = 16
LEVELS = 2
COLS_X = 8
COLS_Y = 16
VOX = 4096
KW = 248832


def draw_active(key, part):
    split_key = jax.random.fold_in(key, 11)
    splits = jax.random.randint(split_key, (COLS_X, COLS_Y // 2), 0, LEVELS + 1)
    pick_x = jax.random.randint(jax.random.fold_in(key, 12), (), 0, COLS_X)
    pick_y = jax.random.randint(jax.random.fold_in(key, 13), (), 0, COLS_Y // 2)
    full_side = LEVELS * jax.random.randint(jax.random.fold_in(key, 14), (), 0, 2)
    splits = splits.at[pick_x, pick_y].set(full_side)
    counts = jnp.stack([splits, LEVELS - splits], axis=-1).reshape(COLS_X, COLS_Y)
    scores = jax.random.randint(jax.random.fold_in(key, 15), (COLS_X, COLS_Y, LEVELS), 0, 1 << 20)
    scores = scores * LEVELS + jnp.arange(LEVELS, dtype=jnp.int32)
    ranks = jnp.argsort(jnp.argsort(scores, axis=-1), axis=-1)
    return (ranks < counts[..., None]).astype(jnp.int32)


def steps_of(own_key, dims, split, smallest, top_value):
    def one(dim, shards_of):
        heights = jax.random.uniform(jax.random.fold_in(jax.random.fold_in(own_key, 6), dim), (shards_of,), jnp.float32, smallest / len(split), top_value / len(split))
        return jnp.repeat(jnp.exp(heights), dims[dim] // shards_of).reshape((-1,) + (1,) * (len(dims) - dim - 1))

    level = one(*split[0])
    for cut in split[1:]:
        level = level * one(*cut)
    return level


def centred(rng, dims, deviation, reach, shards=(), kind=jnp.bfloat16):
    values = deviation * jax.random.normal(rng, dims, jnp.float32)
    if shards:
        values = values * steps_of(rng, dims, shards, -0.22, 0.18)
    return jnp.clip(values, -reach, reach).astype(kind)


def setup_inputs(seed: int = 0) -> dict:
    streams_of = jax.random.split(jax.random.key(seed), 5)
    return {
        "features": centred(streams_of[0], (COLS_X, COLS_Y, LEVELS, C, VOX), 1.0, 6.0, ((0, 8), (1, 16))),
        "grad_out": centred(streams_of[1], (COLS_X, COLS_Y, LEVELS, C, VOX), 1.0, 6.0, ((0, 8), (1, 16))),
        "weight": centred(streams_of[2], (C, 27 * C), (27 * C) ** -0.5, 0.125),
        "active": draw_active(jax.random.fold_in(streams_of[4], 71), 0),
    }


def pad_front(planes, axis_at):
    spread = [(0, 0)] * planes.ndim
    spread[axis_at] = (1, 0)
    return jnp.pad(planes, spread)

def pad_back(planes, axis_at):
    spread = [(0, 0)] * planes.ndim
    spread[axis_at] = (0, 1)
    return jnp.pad(planes, spread)

def reference(features, grad_out, weight, active):
    live_flags = active.astype(jnp.bfloat16)[..., None, None]
    stacked = jnp.stack([features * live_flags, grad_out * live_flags])
    bricks = stacked.reshape(2, COLS_X, COLS_Y, LEVELS, C, EDGE, EDGE, EDGE)
    top_cell = EDGE - 1
    west_rim = pad_front(bricks[:, :-1, :, :, :, top_cell], 1)
    east_rim = pad_back(bricks[:, 1:, :, :, :, 0], 1)
    south_rim = pad_front(bricks[:, :, :-1, :, :, :, top_cell], 2)
    north_rim = pad_back(bricks[:, :, 1:, :, :, :, 0], 2)
    below_rim = pad_front(bricks[:, :, :, :-1, :, :, :, top_cell], 3)
    above_rim = pad_back(bricks[:, :, :, 1:, :, :, :, 0], 3)
    brick_count = COLS_X * COLS_Y * LEVELS

    def by_brick(values):
        moved = jnp.moveaxis(values, 0, 3)
        return moved.reshape((brick_count,) + values.shape[:1] + values.shape[4:])
    brick_items = tuple((by_brick(values) for values in (bricks, west_rim, east_rim, south_rim, north_rim, below_rim, above_rim)))
    brick_items = brick_items + (active.reshape(brick_count),)
    weight_float = weight.astype(jnp.float32).reshape(C, 3, 3, 3, C)
    forward_kernel = jnp.transpose(weight_float, (0, 4, 1, 2, 3))
    backward_kernel = jnp.transpose(weight_float[:, ::-1, ::-1, ::-1, :], (4, 0, 1, 2, 3))
    numbers = ('NCDHW', 'OIDHW', 'NCDHW')

    def brick_step(grad_total, brick_item):
        one_brick, west_side, east_side, south_side, north_side, below_side, above_side, is_live = brick_item

        def compute(unused):
            padded = jnp.pad(one_brick.astype(jnp.float32), ((0, 0), (0, 0), (1, 1), (1, 1), (1, 1)))
            padded = padded.at[:, :, 0, 1:-1, 1:-1].set(west_side.astype(jnp.float32))
            padded = padded.at[:, :, -1, 1:-1, 1:-1].set(east_side.astype(jnp.float32))
            padded = padded.at[:, :, 1:-1, 0, 1:-1].set(south_side.astype(jnp.float32))
            padded = padded.at[:, :, 1:-1, -1, 1:-1].set(north_side.astype(jnp.float32))
            padded = padded.at[:, :, 1:-1, 1:-1, 0].set(below_side.astype(jnp.float32))
            padded = padded.at[:, :, 1:-1, 1:-1, -1].set(above_side.astype(jnp.float32))
            forward_res = lax.conv_general_dilated(padded[0:1], forward_kernel, (1, 1, 1), 'VALID', dimension_numbers=numbers, precision=lax.Precision.HIGHEST)
            backward_res = lax.conv_general_dilated(padded[1:2], backward_kernel, (1, 1, 1), 'VALID', dimension_numbers=numbers, precision=lax.Precision.HIGHEST)
            shifted = jnp.stack([padded[0, :, offset_x:offset_x + EDGE, offset_y:offset_y + EDGE, offset_z:offset_z + EDGE] for offset_x in range(3) for offset_y in range(3) for offset_z in range(3)])
            grad_part = jnp.einsum('cxyz,odxyz->cod', one_brick[1].astype(jnp.float32), shifted, precision=lax.Precision.HIGHEST)
            return (forward_res[0].reshape(C, VOX).astype(jnp.bfloat16), backward_res[0].reshape(C, VOX).astype(jnp.bfloat16), grad_part.reshape(C, 27 * C))

        def skipped(unused):
            return (jnp.zeros((C, VOX), jnp.bfloat16), jnp.zeros((C, VOX), jnp.bfloat16), jnp.zeros((C, 27 * C), jnp.float32))
        result_out, result_grad, grad_part = lax.cond(is_live > 0, compute, skipped, 0)
        return (grad_total + grad_part, (result_out, result_grad))
    start_total = jnp.zeros((C, 27 * C), jnp.float32)
    grad_total, (out_bricks, grad_bricks) = lax.scan(brick_step, start_total, brick_items)
    norm_scale = 1.0 / math.sqrt(brick_count * VOX)
    out = out_bricks.reshape(COLS_X, COLS_Y, LEVELS, C, VOX)
    grad_in = grad_bricks.reshape(COLS_X, COLS_Y, LEVELS, C, VOX)
    return (out, grad_in, (grad_total * norm_scale).reshape(KW))
```

```python
import functools
import math

import jax
import jax.numpy as jnp
from jax import lax
from jax.experimental import pallas as pl
from jax.experimental.pallas import tpu as pltpu
from jax.sharding import PartitionSpec as P

EDGE = 16
PLANE = EDGE * EDGE
NEAR = 9
bf16 = jnp.bfloat16
f32 = jnp.float32


def lanes_of(shape):
    return lax.broadcasted_iota(jnp.int32, shape, 1)


def pick(mask, a, b):
    return jnp.where(mask, a, b)


def pack_kernel(act_ref, f_ref, g_ref, xlo_ref, xhi_ref, ylo_ref, yhi_ref):
    c = f_ref.shape[0]
    live = act_ref[0, 0, pl.program_id(0)].astype(f32).astype(bf16)
    half = lanes_of((c, 128)) // EDGE
    for arr, src in enumerate((f_ref, g_ref)):
        xlo_ref[arr] = src[:, 0:PLANE] * live
        xhi_ref[arr] = src[:, 15 * PLANE : 16 * PLANE] * live
        for h in range(2):
            low = jnp.zeros((c, 128), bf16)
            high = jnp.zeros((c, 128), bf16)
            for xs in range(8):
                x = 8 * h + xs
                a = src[:, x * PLANE : x * PLANE + 128]
                b = src[:, x * PLANE + 128 : x * PLANE + 256]
                if xs:
                    a = pltpu.roll(a, 16 * xs, 1)
                if xs != 7:
                    b = pltpu.roll(b, 16 * xs + 16, 1)
                low = pick(half == xs, a, low)
                high = pick(half == xs, b, high)
            ylo_ref[arr, :, h * 128 : h * 128 + 128] = low * live
            yhi_ref[arr, :, h * 128 : h * 128 + 128] = high * live


def pack(active, features, grads):
    levels, c, vox = features.shape
    face = jax.ShapeDtypeStruct((2, levels, c, PLANE), bf16)
    brick = pl.BlockSpec((None, c, vox), lambda k: (k, 0, 0))
    side = pl.BlockSpec((2, None, c, PLANE), lambda k: (0, k, 0, 0))
    return pl.pallas_call(
        pack_kernel,
        grid=(levels,),
        in_specs=[pl.BlockSpec(memory_space=pltpu.SMEM), brick, brick],
        out_specs=[side] * 4,
        out_shape=[face] * 4,
        name="pack_faces",
    )(active, features, grads)


def shifted_rows(y_ref, lev, ys_ref):
    c = ys_ref.shape[2]
    z = lanes_of((c, PLANE)) % EDGE
    zero = jnp.zeros((c, PLANE), bf16)
    for side in range(2):
        row = y_ref[side, lev]
        ys_ref[side, 0] = pick(z == 0, zero, pltpu.roll(row, 1, 1))
        ys_ref[side, 1] = row
        ys_ref[side, 2] = pick(z == EDGE - 1, zero, pltpu.roll(row, PLANE - 1, 1))


def fill_plane(store, plane, below, above, rows):
    c = plane.shape[0]
    lane = lanes_of((c, PLANE))
    z = lane % EDGE
    down = pltpu.roll(pick(z == EDGE - 1, pltpu.roll(below, PLANE - EDGE, 1), plane), 1, 1)
    up = pltpu.roll(pick(z == 0, pltpu.roll(above, EDGE, 1), plane), PLANE - 1, 1)
    for k, value in enumerate((down, plane, up)):
        south, north = rows(k)
        store(3 + k, value)
        store(k, pltpu.roll(pick(lane >= PLANE - EDGE, south, value), EDGE, 1))
        store(6 + k, pltpu.roll(pick(lane < EDGE, north, value), PLANE - EDGE, 1))


def build_inner(store, act_ref, src_ref, ys_ref, lev, x):
    c = src_ref.shape[1]
    other = 1 - lev
    live = act_ref[0, 0, other].astype(f32)
    start = pl.multiple_of(x * PLANE, PLANE)
    plane = src_ref[lev, :, pl.ds(start, PLANE)]
    beside = src_ref[other, :, pl.ds(start, PLANE)]
    below = beside * (live * lev.astype(f32)).astype(bf16)
    above = beside * (live * other.astype(f32)).astype(bf16)

    def rows(k):
        south = pltpu.roll(ys_ref[0, k], lax.rem(PLANE - EDGE - x * EDGE + PLANE, PLANE), 1)
        north = pltpu.roll(ys_ref[1, k], lax.rem(PLANE - x * EDGE, PLANE), 1)
        return south, north

    fill_plane(store, plane, below, above, rows)


def build_outer(store, plane):
    zero = jnp.zeros_like(plane)
    fill_plane(store, plane, zero, zero, lambda k: (zero, zero))


def conv_kernel(act_ref, src_ref, x_ref, y_ref, w_ref, out_ref, p_ref, ys_ref, acc_ref):
    lev = pl.program_id(0)
    c = src_ref.shape[1]

    @pl.when(act_ref[0, 0, lev] == 0)
    def _():
        out_ref[...] = jnp.zeros_like(out_ref)

    @pl.when(act_ref[0, 0, lev] != 0)
    def _():
        p_ref[NEAR * c :] = jnp.zeros_like(p_ref[NEAR * c :])
        shifted_rows(y_ref, lev, ys_ref)

        def store(at, value):
            p_ref[at * c : (at + 1) * c] = value

        def product():
            return jnp.dot(w_ref[...], p_ref[...], preferred_element_type=f32)

        build_outer(store, x_ref[0, lev])
        acc_ref[0] = product()[:c]
        acc_ref[1] = jnp.zeros_like(acc_ref[1])

        def step(x, _):
            build_inner(store, act_ref, src_ref, ys_ref, lev, x)
            full = product()
            done = acc_ref[1] + full[2 * c :]
            acc_ref[1] = acc_ref[0] + full[c : 2 * c]
            acc_ref[0] = full[:c]

            @pl.when(x > 0)
            def _():
                out_ref[:, pl.ds(pl.multiple_of((x - 1) * PLANE, PLANE), PLANE)] = done.astype(bf16)

            return 0

        lax.fori_loop(0, EDGE, step, 0)
        build_outer(store, x_ref[1, lev])
        full = product()
        out_ref[:, 15 * PLANE :] = (acc_ref[1] + full[2 * c :]).astype(bf16)


def conv(active, src, xface, yface, weight):
    levels, c, vox = src.shape
    depth = weight.shape[1]
    whole = pl.BlockSpec(memory_space=pltpu.VMEM)
    return pl.pallas_call(
        conv_kernel,
        grid=(levels,),
        in_specs=[pl.BlockSpec(memory_space=pltpu.SMEM)] + [whole] * 4,
        out_specs=pl.BlockSpec((None, c, vox), lambda k: (k, 0, 0)),
        out_shape=jax.ShapeDtypeStruct((levels, c, vox), bf16),
        scratch_shapes=[
            pltpu.VMEM((depth, PLANE), bf16),
            pltpu.VMEM((2, 3, c, PLANE), bf16),
            pltpu.VMEM((2, c, PLANE), f32),
        ],
        name="conv",
    )(active, src, xface, yface, weight)


def wgrad_kernel(act_ref, src_ref, grad_ref, x_ref, y_ref, out_ref, p_ref, g_ref, ys_ref):
    c = src_ref.shape[1]
    planes = EDGE + 2

    out_ref[...] = jnp.zeros_like(out_ref)
    p_ref[NEAR * c :] = jnp.zeros_like(p_ref[NEAR * c :])
    g_ref[...] = jnp.zeros_like(g_ref)

    def level(lev, _):
        @pl.when(act_ref[0, 0, lev] != 0)
        def _():
            shifted_rows(y_ref, lev, ys_ref)

            def store_at(start):
                def store(at, value):
                    p_ref[at * c : (at + 1) * c, pl.ds(start, PLANE)] = value

                return store

            for dx in range(3):
                g_ref[dx * c : (dx + 1) * c, dx * PLANE : (dx + EDGE) * PLANE] = grad_ref[lev]
            build_outer(store_at(0), x_ref[0, lev])

            def step(x, _):
                start = pl.multiple_of((x + 1) * PLANE, PLANE)
                build_inner(store_at(start), act_ref, src_ref, ys_ref, lev, x)
                return 0

            lax.fori_loop(0, EDGE, step, 0)
            build_outer(store_at((EDGE + 1) * PLANE), x_ref[1, lev])

            def gather(at, _):
                cells = pl.ds(pl.multiple_of(at * 3 * PLANE, 3 * PLANE), 3 * PLANE)
                out_ref[...] += lax.dot_general(
                    g_ref[:, cells],
                    p_ref[:, cells],
                    (((1,), (1,)), ((), ())),
                    preferred_element_type=f32,
                )
                return 0

            lax.fori_loop(0, planes // 3, gather, 0)

        return 0

    lax.fori_loop(0, 2, level, 0)


def wgrad(active, src, grads, xface, yface, depth):
    levels, c, vox = src.shape
    whole = pl.BlockSpec(memory_space=pltpu.VMEM)
    wide = (EDGE + 2) * PLANE
    return pl.pallas_call(
        wgrad_kernel,
        in_specs=[pl.BlockSpec(memory_space=pltpu.SMEM)] + [whole] * 4,
        out_specs=whole,
        out_shape=jax.ShapeDtypeStruct((3 * c, depth), f32),
        scratch_shapes=[
            pltpu.VMEM((depth, wide), bf16),
            pltpu.VMEM((3 * c, wide), bf16),
            pltpu.VMEM((2, 3, c, PLANE), bf16),
        ],
        name="wgrad",
    )(active, src, grads, xface, yface)


def neighbours(low, high, axis):
    count = lax.axis_size(axis)
    forward = [(i, i + 1) for i in range(count - 1)]
    backward = [(j, i) for i, j in forward]
    return lax.ppermute(high, axis, forward), lax.ppermute(low, axis, backward)


def body(features, grad_out, weight, active):
    levels, c, vox = features.shape[2:]
    depth = -(-NEAR * c // 128) * 128
    fields = features.reshape(levels, c, vox)
    grads = grad_out.reshape(levels, c, vox)
    xlo, xhi, ylo, yhi = pack(active, fields, grads)
    west, east = neighbours(xlo, xhi, "gx")
    south, north = neighbours(ylo, yhi, "gy")
    xfaces = jnp.stack([west, east], axis=1)
    yfaces = jnp.stack([south, north], axis=1)

    cube = weight.reshape(c, 3, NEAR, c)
    fill = ((0, 0), (0, depth - NEAR * c))
    ahead = jnp.pad(cube.transpose(1, 0, 2, 3).reshape(3 * c, NEAR * c), fill)
    back = jnp.pad(
        cube[:, ::-1, ::-1].transpose(1, 3, 2, 0).reshape(3 * c, NEAR * c), fill
    )

    gw = wgrad(active, fields, grads, xfaces[0], yfaces[0], depth)
    parts = lax.axis_size("gx") * lax.axis_size("gy")
    flat = gw[:, : NEAR * c].reshape(3, c, NEAR * c).transpose(1, 0, 2).reshape(parts, -1)
    share = flat.shape[1]
    rows = -(-share // 1024) * 8
    flat = jnp.pad(flat, ((0, 0), (0, rows * 128 - share))).reshape(parts, rows, 128)
    swapped = lax.all_to_all(flat, ("gx", "gy"), 0, 0, tiled=True)
    norm_scale = 1.0 / math.sqrt(parts * levels * vox)
    summed = swapped.sum(0).reshape(-1)[:share] * norm_scale

    out = conv(active, fields, xfaces[0], yfaces[0], ahead)
    grad_in = conv(active, grads, xfaces[1], yfaces[1], back)
    return out[None, None], grad_in[None, None], summed


def solution(mesh):
    placed = (
        P("gx", "gy", None, None, None),
        P("gx", "gy", None, None, None),
        P(),
        P("gx", "gy", None),
    )
    return jax.shard_map(
        body,
        mesh=mesh,
        in_specs=placed,
        out_specs=(
            P("gx", "gy", None, None, None),
            P("gx", "gy", None, None, None),
            P(("gx", "gy")),
        ),
        check_vma=False,
    )
```

```python
import functools
import math

import jax
import jax.numpy as jnp
from jax import lax
from jax.experimental import pallas as pl
from jax.experimental.pallas import tpu as pltpu
from jax.sharding import PartitionSpec as P

EDGE = 16
PLANE = EDGE * EDGE
NEAR = 9
bf16 = jnp.bfloat16
f32 = jnp.float32


def lanes_of(shape):
    return lax.broadcasted_iota(jnp.int32, shape, 1)


def pick(mask, a, b):
    return jnp.where(mask, a, b)


def pack_kernel(act_ref, f_ref, g_ref, xlo_ref, xhi_ref, ylo_ref, yhi_ref):
    c = f_ref.shape[0]
    live = act_ref[0, 0, pl.program_id(0)].astype(f32).astype(bf16)
    half = lanes_of((c, 128)) // EDGE
    for arr, src in enumerate((f_ref, g_ref)):
        xlo_ref[arr] = src[:, 0:PLANE] * live
        xhi_ref[arr] = src[:, 15 * PLANE : 16 * PLANE] * live
        for h in range(2):
            low = jnp.zeros((c, 128), bf16)
            high = jnp.zeros((c, 128), bf16)
            for xs in range(8):
                x = 8 * h + xs
                a = src[:, x * PLANE : x * PLANE + 128]
                b = src[:, x * PLANE + 128 : x * PLANE + 256]
                if xs:
                    a = pltpu.roll(a, 16 * xs, 1)
                if xs != 7:
                    b = pltpu.roll(b, 16 * xs + 16, 1)
                low = pick(half == xs, a, low)
                high = pick(half == xs, b, high)
            ylo_ref[arr, :, h * 128 : h * 128 + 128] = low * live
            yhi_ref[arr, :, h * 128 : h * 128 + 128] = high * live


def pack(active, features, grads):
    levels, c, vox = features.shape
    face = jax.ShapeDtypeStruct((2, levels, c, PLANE), bf16)
    brick = pl.BlockSpec((None, c, vox), lambda k: (k, 0, 0))
    side = pl.BlockSpec((2, None, c, PLANE), lambda k: (0, k, 0, 0))
    return pl.pallas_call(
        pack_kernel,
        grid=(levels,),
        in_specs=[pl.BlockSpec(memory_space=pltpu.SMEM), brick, brick],
        out_specs=[side] * 4,
        out_shape=[face] * 4,
        name="pack_faces",
    )(active, features, grads)


def z_moved(value, mask, fill, amount):
    return pick(mask, fill, pltpu.roll(value, amount, 1))


def fill_plane(store, halves, fills, edge):
    c = halves[0].shape[0]
    lane = lanes_of((c, 128))
    z = lane % EDGE
    zero = jnp.zeros((c, 128), bf16)
    below, above = fills
    moved = (
        [z_moved(v, z == 0, f, 1) for v, f in zip(halves, below)],
        halves,
        [z_moved(v, z == EDGE - 1, f, 127) for v, f in zip(halves, above)],
    )
    if edge is None:
        rows = (zero,) * 3
    else:
        rows = (z_moved(edge, z == 0, zero, 1), edge, z_moved(edge, z == EDGE - 1, zero, 127))
    for k in range(3):
        first, last = moved[k]
        store(3 + k, 0, first)
        store(3 + k, 1, last)
        first_on, last_on = pltpu.roll(first, EDGE, 1), pltpu.roll(last, EDGE, 1)
        store(k, 0, pick(lane < EDGE, rows[k], first_on))
        store(k, 1, pick(lane < EDGE, first_on, last_on))
        first_off, last_off = (pltpu.roll(v, 128 - EDGE, 1) for v in (first, last))
        store(6 + k, 0, pick(lane >= 128 - EDGE, last_off, first_off))
        store(6 + k, 1, pick(lane >= 128 - EDGE, rows[k], last_off))


def build_inner(store, act_ref, src_ref, y_ref, lev, x):
    c = src_ref.shape[1]
    other = 1 - lev
    live = act_ref[0, 0, other]
    start = pl.multiple_of(x * PLANE, PLANE)
    halves = [src_ref[lev, :, pl.ds(start + h, 128)] for h in (0, 128)]
    turn = EDGE - 1 + lev * (128 - 2 * (EDGE - 1))
    beside = [pltpu.roll(src_ref[other, :, pl.ds(start + h, 128)], turn, 1) for h in (0, 128)]
    below_on = (live * lev).astype(f32).astype(bf16)
    above_on = (live * other).astype(f32).astype(bf16)
    below = [v * below_on for v in beside]
    above = [v * above_on for v in beside]
    at = pl.multiple_of((x // 8) * 128, 128)
    back = 16 * lax.rem(x, 8)
    south = pltpu.roll(y_ref[0, lev, :, pl.ds(at, 128)], lax.rem(128 - back, 128), 1)
    north = pltpu.roll(y_ref[1, lev, :, pl.ds(at, 128)], 112 - back, 1)
    edge = pick(lanes_of((c, 128)) < EDGE, south, north)
    fill_plane(store, halves, (below, above), edge)


def build_outer(store, plane):
    zero = jnp.zeros((plane.shape[0], 128), bf16)
    fill_plane(store, [plane[:, :128], plane[:, 128:]], ([zero] * 2,) * 2, None)


def storing(p_ref, c, start=0):
    def store(at, half, value):
        p_ref[at * c : (at + 1) * c, start + half * 128 : start + half * 128 + 128] = value

    return store


def conv_kernel(act_ref, src_ref, x_ref, y_ref, w_ref, out_ref, pa_ref, pb_ref, acc_ref):
    lev = pl.program_id(0)
    c = src_ref.shape[1]

    @pl.when(act_ref[0, 0, lev] == 0)
    def _():
        out_ref[...] = jnp.zeros_like(out_ref)

    @pl.when(act_ref[0, 0, lev] != 0)
    def _():
        def inner(p_ref, x):
            build_inner(storing(p_ref, c), act_ref, src_ref, y_ref, lev, x)

        def product(p_ref):
            return jnp.dot(w_ref[...], p_ref[...], preferred_element_type=f32)

        def advance(p_ref, x):
            full = product(p_ref)
            done = acc_ref[1] + full[2 * c :]
            acc_ref[1] = acc_ref[0] + full[c : 2 * c]
            acc_ref[0] = full[:c]
            start = pl.multiple_of(jnp.maximum(x - 1, 0) * PLANE, PLANE)
            out_ref[:, pl.ds(start, PLANE)] = done.astype(bf16)

        for p_ref in (pa_ref, pb_ref):
            p_ref[NEAR * c :] = jnp.zeros_like(p_ref[NEAR * c :])
        acc_ref[...] = jnp.zeros_like(acc_ref)
        build_outer(storing(pa_ref, c), x_ref[0, lev])

        def step(j, _):
            x = 2 * j
            inner(pb_ref, x)
            advance(pa_ref, x - 1)
            inner(pa_ref, x + 1)
            advance(pb_ref, x)
            return 0

        lax.fori_loop(0, EDGE // 2, step, 0)
        build_outer(storing(pb_ref, c), x_ref[1, lev])
        advance(pa_ref, EDGE - 1)
        advance(pb_ref, EDGE)


def conv(active, src, xface, yface, weight):
    levels, c, vox = src.shape
    depth = weight.shape[1]
    whole = pl.BlockSpec(memory_space=pltpu.VMEM)
    return pl.pallas_call(
        conv_kernel,
        grid=(levels,),
        in_specs=[pl.BlockSpec(memory_space=pltpu.SMEM)] + [whole] * 4,
        out_specs=pl.BlockSpec((None, c, vox), lambda k: (k, 0, 0)),
        out_shape=jax.ShapeDtypeStruct((levels, c, vox), bf16),
        scratch_shapes=[
            pltpu.VMEM((depth, PLANE), bf16),
            pltpu.VMEM((depth, PLANE), bf16),
            pltpu.VMEM((2, c, PLANE), f32),
        ],
        name="conv",
    )(active, src, xface, yface, weight)


CHUNK = 3


def wgrad_kernel(act_ref, src_ref, grad_ref, x_ref, y_ref, out_ref, pa_ref, pb_ref, g_ref):
    c = src_ref.shape[1]
    chunks = (EDGE + 2) // CHUNK
    wide = CHUNK * PLANE
    out_ref[...] = jnp.zeros_like(out_ref)
    for p_ref in (pa_ref, pb_ref):
        p_ref[NEAR * c :] = jnp.zeros_like(p_ref[NEAR * c :])
    g_ref[:, : 2 * PLANE] = jnp.zeros((c, 2 * PLANE), bf16)
    g_ref[:, (EDGE + 2) * PLANE :] = jnp.zeros((c, 2 * PLANE), bf16)

    def level(lev, _):
        @pl.when(act_ref[0, 0, lev] != 0)
        def _():
            g_ref[:, 2 * PLANE : (EDGE + 2) * PLANE] = grad_ref[lev]

            def fill(p_ref, at, first=False, last=False):
                for n in range(CHUNK):
                    store = storing(p_ref, c, n * PLANE)
                    if first and n == 0:
                        build_outer(store, x_ref[0, lev])
                    elif last and n == CHUNK - 1:
                        build_outer(store, x_ref[1, lev])
                    else:
                        build_inner(store, act_ref, src_ref, y_ref, lev, at * CHUNK + n - 1)

            def gather(p_ref, at):
                moved = [
                    g_ref[:, pl.ds(pl.multiple_of((at * CHUNK + 2 - dx) * PLANE, PLANE), wide)]
                    for dx in range(3)
                ]
                out_ref[...] += lax.dot_general(
                    jnp.concatenate(moved, axis=0),
                    p_ref[...],
                    (((1,), (1,)), ((), ())),
                    preferred_element_type=f32,
                )

            fill(pa_ref, jnp.int32(0), first=True)

            def step(j, _):
                fill(pb_ref, 2 * j + 1)
                gather(pa_ref, 2 * j)
                fill(pa_ref, 2 * j + 2)
                gather(pb_ref, 2 * j + 1)
                return 0

            lax.fori_loop(0, chunks // 2 - 1, step, 0)
            fill(pb_ref, jnp.int32(chunks - 1), last=True)
            gather(pa_ref, jnp.int32(chunks - 2))
            gather(pb_ref, jnp.int32(chunks - 1))

        return 0

    lax.fori_loop(0, 2, level, 0)


def wgrad(active, src, grads, xface, yface, depth):
    levels, c, vox = src.shape
    whole = pl.BlockSpec(memory_space=pltpu.VMEM)
    return pl.pallas_call(
        wgrad_kernel,
        in_specs=[pl.BlockSpec(memory_space=pltpu.SMEM)] + [whole] * 4,
        out_specs=whole,
        out_shape=jax.ShapeDtypeStruct((3 * c, depth), f32),
        scratch_shapes=[
            pltpu.VMEM((depth, CHUNK * PLANE), bf16),
            pltpu.VMEM((depth, CHUNK * PLANE), bf16),
            pltpu.VMEM((c, (EDGE + 4) * PLANE), bf16),
        ],
        name="wgrad",
    )(active, src, grads, xface, yface)


def neighbours(low, high, axis):
    count = lax.axis_size(axis)
    forward = [(i, i + 1) for i in range(count - 1)]
    backward = [(j, i) for i, j in forward]
    return lax.ppermute(high, axis, forward), lax.ppermute(low, axis, backward)


def body(features, grad_out, weight, active):
    levels, c, vox = features.shape[2:]
    depth = -(-NEAR * c // 128) * 128
    fields = features.reshape(levels, c, vox)
    grads = grad_out.reshape(levels, c, vox)
    xlo, xhi, ylo, yhi = pack(active, fields, grads)
    west, east = neighbours(xlo, xhi, "gx")
    south, north = neighbours(ylo, yhi, "gy")
    xfaces = jnp.stack([west, east], axis=1)
    yfaces = jnp.stack([south, north], axis=1)

    cube = weight.reshape(c, 3, NEAR, c)
    fill = ((0, 0), (0, depth - NEAR * c))
    ahead = jnp.pad(cube.transpose(1, 0, 2, 3).reshape(3 * c, NEAR * c), fill)
    back = jnp.pad(
        cube[:, ::-1, ::-1].transpose(1, 3, 2, 0).reshape(3 * c, NEAR * c), fill
    )

    gw = wgrad(active, fields, grads, xfaces[0], yfaces[0], depth)
    parts = lax.axis_size("gx") * lax.axis_size("gy")
    flat = gw[:, : NEAR * c].reshape(3, c, NEAR * c).transpose(1, 0, 2).reshape(parts, -1)
    share = flat.shape[1]
    rows = -(-share // 1024) * 8
    flat = jnp.pad(flat, ((0, 0), (0, rows * 128 - share))).reshape(parts, rows, 128)
    swapped = lax.all_to_all(flat, ("gx", "gy"), 0, 0, tiled=True)
    norm_scale = 1.0 / math.sqrt(parts * levels * vox)
    summed = swapped.sum(0).reshape(-1)[:share] * norm_scale

    out = conv(active, fields, xfaces[0], yfaces[0], ahead)
    grad_in = conv(active, grads, xfaces[1], yfaces[1], back)
    return out[None, None], grad_in[None, None], summed


def solution(mesh):
    placed = (
        P("gx", "gy", None, None, None),
        P("gx", "gy", None, None, None),
        P(),
        P("gx", "gy", None),
    )
    return jax.shard_map(
        body,
        mesh=mesh,
        in_specs=placed,
        out_specs=(
            P("gx", "gy", None, None, None),
            P("gx", "gy", None, None, None),
            P(("gx", "gy")),
        ),
        check_vma=False,
    )
```

```python
import functools
import math

import jax
import jax.numpy as jnp
from jax import lax
from jax.experimental import pallas as pl
from jax.experimental.pallas import tpu as pltpu
from jax.sharding import PartitionSpec as P

EDGE = 16
CONV_CHUNK = 3
CHUNK = 4
PLANE = EDGE * EDGE
NEAR = 9
bf16 = jnp.bfloat16
f32 = jnp.float32


def lanes_of(shape):
    return lax.broadcasted_iota(jnp.int32, shape, 1)


def pick(mask, a, b):
    return jnp.where(mask, a, b)


def pack_kernel(act_ref, f_ref, g_ref, xlo_ref, xhi_ref, ylo_ref, yhi_ref):
    c = f_ref.shape[0]
    live = act_ref[0, 0, pl.program_id(0)].astype(f32).astype(bf16)
    half = lanes_of((c, 128)) // EDGE
    for arr, src in enumerate((f_ref, g_ref)):
        xlo_ref[arr] = src[:, 0:PLANE] * live
        xhi_ref[arr] = src[:, 15 * PLANE : 16 * PLANE] * live
        for h in range(2):
            low = jnp.zeros((c, 128), bf16)
            high = jnp.zeros((c, 128), bf16)
            for xs in range(8):
                x = 8 * h + xs
                a = src[:, x * PLANE : x * PLANE + 128]
                b = src[:, x * PLANE + 128 : x * PLANE + 256]
                if xs:
                    a = pltpu.roll(a, 16 * xs, 1)
                if xs != 7:
                    b = pltpu.roll(b, 16 * xs + 16, 1)
                low = pick(half == xs, a, low)
                high = pick(half == xs, b, high)
            ylo_ref[arr, :, h * 128 : h * 128 + 128] = low * live
            yhi_ref[arr, :, h * 128 : h * 128 + 128] = high * live


def pack(active, features, grads):
    levels, c, vox = features.shape
    face = jax.ShapeDtypeStruct((2, levels, c, PLANE), bf16)
    brick = pl.BlockSpec((None, c, vox), lambda k: (k, 0, 0))
    side = pl.BlockSpec((2, None, c, PLANE), lambda k: (0, k, 0, 0))
    return pl.pallas_call(
        pack_kernel,
        grid=(levels,),
        in_specs=[pl.BlockSpec(memory_space=pltpu.SMEM), brick, brick],
        out_specs=[side] * 4,
        out_shape=[face] * 4,
        name="pack_faces",
    )(active, features, grads)


def turned(value, amount):
    return pltpu.roll(value, amount % 128, 1) if amount % 128 else value


def z_moved(value, mask, fill, amount):
    return pick(mask, fill, pltpu.roll(value, amount, 1))


def fill_plane(store, halves, fills, edge):
    c = halves[0].shape[0]
    lane = lanes_of((c, 128))
    z = lane % EDGE
    zero = jnp.zeros((c, 128), bf16)
    below, above = fills
    moved = (
        [z_moved(v, z == 0, f, 1) for v, f in zip(halves, below)],
        halves,
        [z_moved(v, z == EDGE - 1, f, 127) for v, f in zip(halves, above)],
    )
    if edge is None:
        rows = (zero,) * 3
    else:
        rows = (z_moved(edge, z == 0, zero, 1), edge, z_moved(edge, z == EDGE - 1, zero, 127))
    for k in range(3):
        first, last = moved[k]
        store(3 + k, 0, first)
        store(3 + k, 1, last)
        first_on, last_on = pltpu.roll(first, EDGE, 1), pltpu.roll(last, EDGE, 1)
        store(k, 0, pick(lane < EDGE, rows[k], first_on))
        store(k, 1, pick(lane < EDGE, first_on, last_on))
        first_off, last_off = (pltpu.roll(v, 128 - EDGE, 1) for v in (first, last))
        store(6 + k, 0, pick(lane >= 128 - EDGE, last_off, first_off))
        store(6 + k, 1, pick(lane >= 128 - EDGE, rows[k], last_off))


def build_inner(store, act_ref, src_ref, y_refs, arr, lev, x):
    c = src_ref.shape[1]
    other = 1 - lev
    live = act_ref[0, 0, other]
    start = x * PLANE
    halves = [src_ref[lev, :, pl.ds(start + h, 128)] for h in (0, 128)]
    turn = EDGE - 1 + lev * (128 - 2 * (EDGE - 1))
    beside = [pltpu.roll(src_ref[other, :, pl.ds(start + h, 128)], turn, 1) for h in (0, 128)]
    below_on = (live * lev).astype(f32).astype(bf16)
    above_on = (live * other).astype(f32).astype(bf16)
    below = [v * below_on for v in beside]
    above = [v * above_on for v in beside]
    edge = None
    if y_refs is not None:
        at = (x // 8) * 128
        back = EDGE * (x % 8)
        south, north = (r[arr, lev, :, at : at + 128] for r in y_refs)
        south, north = turned(south, -back), turned(north, 112 - back)
        edge = pick(lanes_of((c, 128)) < EDGE, south, north)
    fill_plane(store, halves, (below, above), edge)


def build_outer(store, plane):
    zero = jnp.zeros((plane.shape[0], 128), bf16)
    fill_plane(store, [plane[:, :128], plane[:, 128:]], ([zero] * 2,) * 2, None)


def storing(p_ref, c, start=0):
    def store(at, half, value):
        p_ref[at * c : (at + 1) * c, start + half * 128 : start + half * 128 + 128] = value

    return store


def conv_kernel(
    act_ref, f_ref, g_ref, xw_ref, xe_ref, ys_ref, yn_ref, w_ref, out_ref, back_ref,
    src_ref, pa_ref, pb_ref, acc_ref, res_ref, in_sem, out_sem,
):
    c = src_ref.shape[2]
    levels = src_ref.shape[1]
    chunks = (EDGE + 2) // CONV_CHUNK
    loads = [pltpu.make_async_copy(r, src_ref.at[i], in_sem.at[i]) for i, r in enumerate((f_ref, g_ref))]
    for load in loads:
        load.start()
    bufs = (pa_ref, pb_ref)
    for p_ref in bufs:
        p_ref[NEAR * c :] = jnp.zeros_like(p_ref[NEAR * c :])

    def save(arr, lev, start):
        slot = lax.rem(lev, 2)
        for i, to in enumerate((out_ref, back_ref)):

            @pl.when(arr == i)
            def _():
                copy = pltpu.make_async_copy(res_ref.at[slot], to.at[lev], out_sem.at[slot])
                copy.start() if start else copy.wait()

    def brick(item, _):
        arr, lev = item // levels, lax.rem(item, levels)
        slot = lax.rem(lev, 2)

        for i, load in enumerate(loads):

            @pl.when(item == i * levels)
            def _():
                load.wait()

        @pl.when(item >= 2)
        def _():
            save((item - 2) // levels, lax.rem(item - 2, levels), False)

        @pl.when(act_ref[0, 0, lev] == 0)
        def _():
            res_ref[slot] = jnp.zeros_like(res_ref[slot])

        @pl.when(act_ref[0, 0, lev] != 0)
        def _():
            def fill(p_ref, at):
                for n in range(CONV_CHUNK):
                    x = at * CONV_CHUNK + n - 1
                    store = storing(p_ref, c, n * PLANE)
                    if x < 0 or x == EDGE:
                        build_outer(store, (xw_ref if x < 0 else xe_ref)[arr, lev])
                    else:
                        build_inner(store, act_ref, src_ref.at[arr], (ys_ref, yn_ref), arr, lev, x)

            def advance(p_ref, at):
                full = jnp.dot(w_ref[arr], p_ref[...], preferred_element_type=f32)
                held = [acc_ref[0], acc_ref[1], None] if at else [None] * 3
                for n in range(CONV_CHUNK):
                    x = at * CONV_CHUNK + n - 1
                    lanes = slice(n * PLANE, (n + 1) * PLANE)
                    for dx in range(3):
                        term = full[dx * c : (dx + 1) * c, lanes]
                        i = 2 - dx
                        held[i] = term if held[i] is None else held[i] + term
                    if x > 0:
                        res_ref[slot, :, (x - 1) * PLANE : x * PLANE] = held[0].astype(bf16)
                    held = held[1:] + [None]
                acc_ref[0] = held[0]
                acc_ref[1] = held[1]

            fill(bufs[0], 0)
            for at in range(chunks):
                if at + 1 < chunks:
                    fill(bufs[(at + 1) % 2], at + 1)
                advance(bufs[at % 2], at)

        save(arr, lev, True)
        return 0

    lax.fori_loop(0, 2 * levels, brick, 0)
    for lev in range(levels - 2, levels):
        save(1, lev, False)


def conv(active, fields, grads, faces, weights):
    levels, c, vox = fields.shape
    depth = weights.shape[2]
    whole = pl.BlockSpec(memory_space=pltpu.VMEM)
    apart = pl.BlockSpec(memory_space=pl.ANY)
    return pl.pallas_call(
        conv_kernel,
        in_specs=[pl.BlockSpec(memory_space=pltpu.SMEM)] + [apart] * 2 + [whole] * 5,
        out_specs=[apart] * 2,
        out_shape=[jax.ShapeDtypeStruct((levels, c, vox), bf16)] * 2,
        scratch_shapes=[
            pltpu.VMEM((2, levels, c, vox), bf16),
            pltpu.VMEM((depth, CONV_CHUNK * PLANE), bf16),
            pltpu.VMEM((depth, CONV_CHUNK * PLANE), bf16),
            pltpu.VMEM((2, c, PLANE), f32),
            pltpu.VMEM((2, c, vox), bf16),
            pltpu.SemaphoreType.DMA((2,)),
            pltpu.SemaphoreType.DMA((2,)),
        ],
        name="conv",
    )(active, fields, grads, *faces, weights)


def wgrad_kernel(act_ref, src_ref, grad_ref, out_ref, pa_ref, pb_ref, g_ref):
    c = src_ref.shape[1]
    chunks = EDGE // CHUNK
    wide = CHUNK * PLANE
    out_ref[...] = jnp.zeros_like(out_ref)
    bufs = (pa_ref, pb_ref)
    for p_ref in bufs:
        p_ref[NEAR * c :] = jnp.zeros_like(p_ref[NEAR * c :])
    g_ref[:, :PLANE] = jnp.zeros((c, PLANE), bf16)
    g_ref[:, (EDGE + 1) * PLANE :] = jnp.zeros((c, PLANE), bf16)

    def level(lev, _):
        @pl.when(act_ref[0, 0, lev] != 0)
        def _():
            g_ref[:, PLANE : (EDGE + 1) * PLANE] = grad_ref[lev]

            def fill(p_ref, at):
                for n in range(CHUNK):
                    store = storing(p_ref, c, n * PLANE)
                    build_inner(store, act_ref, src_ref, None, 0, lev, at * CHUNK + n)

            def gather(p_ref, at):
                starts = [(at * CHUNK + 2 - dx) * PLANE for dx in range(3)]
                out_ref[...] += lax.dot_general(
                    jnp.concatenate([g_ref[:, i : i + wide] for i in starts], axis=0),
                    p_ref[...],
                    (((1,), (1,)), ((), ())),
                    preferred_element_type=f32,
                )

            fill(bufs[0], 0)
            for at in range(chunks):
                if at + 1 < chunks:
                    fill(bufs[(at + 1) % 2], at + 1)
                gather(bufs[at % 2], at)

        return 0

    lax.fori_loop(0, 2, level, 0)


def wgrad(active, src, grads, depth):
    levels, c, vox = src.shape
    whole = pl.BlockSpec(memory_space=pltpu.VMEM)
    return pl.pallas_call(
        wgrad_kernel,
        in_specs=[pl.BlockSpec(memory_space=pltpu.SMEM)] + [whole] * 2,
        out_specs=whole,
        out_shape=jax.ShapeDtypeStruct((3 * c, depth), f32),
        scratch_shapes=[
            pltpu.VMEM((depth, CHUNK * PLANE), bf16),
            pltpu.VMEM((depth, CHUNK * PLANE), bf16),
            pltpu.VMEM((c, (EDGE + 2) * PLANE), bf16),
        ],
        name="wgrad",
    )(active, src, grads)


def rim_kernel(
    sum_ref, gxl_ref, gxh_ref, gyl_ref, gyh_ref, xw_ref, xe_ref, ys_ref, yn_ref,
    out_ref, px_ref, py_ref,
):
    c = gxl_ref.shape[2]
    levels = gxl_ref.shape[1]
    px_ref[:, NEAR * c :] = jnp.zeros_like(px_ref[:, NEAR * c :])
    py_ref[...] = jnp.zeros_like(py_ref)

    def both(ref):
        return jnp.concatenate([ref[1, k] for k in range(levels)], axis=1)

    def gathered(left, right):
        return lax.dot_general(left, right, (((1,), (1,)), ((), ())), preferred_element_type=f32)

    for side, halo in enumerate((xw_ref, xe_ref)):
        for k in range(levels):
            build_outer(storing(px_ref.at[side], c, k * PLANE), halo[0, k])
    for side, halo in enumerate((ys_ref, yn_ref)):
        for k in range(levels):

            def store(at, half, value):
                row = 64 * side + (at % 3) * c
                col = k * PLANE + half * 128
                py_ref[side, at // 3, row : row + c, col : col + 128] = value

            build_outer(store, halo[0, k])
    split = py_ref.shape[2]
    far = out_ref.shape[1] - split
    for dx in range(3):
        rows = slice(dx * c, (dx + 1) * c)
        total = sum_ref[rows]
        if dx != 1:
            own = gxl_ref if dx == 0 else gxh_ref
            total = total + gathered(both(own), px_ref[dx // 2])
        low = total[:, :split] + gathered(both(gyl_ref), py_ref[0, dx])
        high = total[:, far:] + gathered(both(gyh_ref), py_ref[1, dx])
        out_ref[rows, :split] = low
        out_ref[rows, split:far] = total[:, split:far]
        out_ref[rows, far:] = high


def rim(sums, own, halos):
    levels, c = own[0].shape[1:3]
    depth = sums.shape[1]
    whole = pl.BlockSpec(memory_space=pltpu.VMEM)
    return pl.pallas_call(
        rim_kernel,
        in_specs=[whole] * 9,
        out_specs=whole,
        out_shape=jax.ShapeDtypeStruct(sums.shape, f32),
        scratch_shapes=[
            pltpu.VMEM((2, depth, levels * PLANE), bf16),
            pltpu.VMEM((2, 3, 384, levels * PLANE), bf16),
        ],
        name="rim",
    )(sums, *own, *halos)


def neighbours(low, high, axis):
    count = lax.axis_size(axis)
    forward = [(i, i + 1) for i in range(count - 1)]
    backward = [(j, i) for i, j in forward]
    return lax.ppermute(high, axis, forward), lax.ppermute(low, axis, backward)


def body(features, grad_out, weight, active):
    levels, c, vox = features.shape[2:]
    depth = -(-NEAR * c // 128) * 128
    fields = features.reshape(levels, c, vox)
    grads = grad_out.reshape(levels, c, vox)
    own = pack(active, fields, grads)
    halos = neighbours(own[0], own[1], "gx") + neighbours(own[2], own[3], "gy")

    cube = weight.reshape(c, 3, NEAR, c)
    ahead = cube.transpose(1, 0, 2, 3)
    back = cube[:, ::-1, ::-1].transpose(1, 3, 2, 0)
    both = jnp.stack([ahead, back]).reshape(2, 3 * c, NEAR * c)
    both = jnp.pad(both, ((0, 0), (0, 0), (0, depth - NEAR * c)))

    gw = rim(wgrad(active, fields, grads, depth), own, halos)
    parts = lax.axis_size("gx") * lax.axis_size("gy")
    flat = gw[:, : NEAR * c].reshape(3, c, NEAR * c).transpose(1, 0, 2).reshape(parts, -1)
    share = flat.shape[1]
    rows = -(-share // 1024) * 8
    flat = jnp.pad(flat, ((0, 0), (0, rows * 128 - share))).reshape(parts, rows, 128)
    swapped = lax.all_to_all(flat, ("gx", "gy"), 0, 0, tiled=True)
    norm_scale = 1.0 / math.sqrt(parts * levels * vox)
    summed = swapped.sum(0).reshape(-1)[:share] * norm_scale

    out, grad_in = conv(active, fields, grads, halos, both)
    return out[None, None], grad_in[None, None], summed


def solution(mesh):
    placed = (
        P("gx", "gy", None, None, None),
        P("gx", "gy", None, None, None),
        P(),
        P("gx", "gy", None),
    )
    return jax.shard_map(
        body,
        mesh=mesh,
        in_specs=placed,
        out_specs=(
            P("gx", "gy", None, None, None),
            P("gx", "gy", None, None, None),
            P(("gx", "gy")),
        ),
        check_vma=False,
    )
```

```python
import functools
import math

import jax
import jax.numpy as jnp
from jax import lax
from jax.experimental import pallas as pl
from jax.experimental.pallas import tpu as pltpu
from jax.sharding import PartitionSpec as P

EDGE = 16
CONV_CHUNK = 3
GRANT = 20 << 20
CHUNK = 4
PLANE = EDGE * EDGE
NEAR = 9
bf16 = jnp.bfloat16
f32 = jnp.float32


def lanes_of(shape):
    return lax.broadcasted_iota(jnp.int32, shape, 1)


def pick(mask, a, b):
    return jnp.where(mask, a, b)


def spread_weight(weight_ref, w_ref, wide_ref, turn_ref):
    c, count = weight_ref.shape
    depth = w_ref.shape[2]
    wide_ref[:, wide_ref.shape[1] - 128 :] = jnp.zeros((c, 128), bf16)
    wide_ref[:, :count] = weight_ref[...]
    inside = lanes_of((c, depth)) < NEAR * c
    lane = lanes_of((c, 128))
    eye = (lane == lax.broadcasted_iota(jnp.int32, (c, 128), 0)).astype(f32).astype(bf16)
    for dx in range(3):
        start = dx * NEAR * c
        tile = start // 128 * 128
        value = wide_ref[:, tile : tile + (depth if dx == 0 else depth + 128)]
        if dx:
            value = pltpu.roll(value, depth + 128 - (start - tile), 1)[:, :depth]
        w_ref[0, dx * c : (dx + 1) * c] = pick(inside, value, jnp.zeros((c, depth), bf16))
        for near in range(NEAR):
            start = (3 * NEAR - 1 - dx * NEAR - near) * c
            tile, off = start // 128 * 128, start % 128
            value = turned(wide_ref[:, tile : tile + 128], -off)
            if off + c > 128:
                after = turned(wide_ref[:, tile + 128 : tile + 256], -off)
                value = pick(lane < 128 - off, value, after)
            turn_ref[dx, near * c : (near + 1) * c] = value
        turn_ref[dx, NEAR * c :] = jnp.zeros((depth - NEAR * c, 128), bf16)
        swapped = lax.dot_general(
            eye, turn_ref[dx], (((1,), (1,)), ((), ())), preferred_element_type=f32
        )
        w_ref[1, dx * c : (dx + 1) * c] = swapped.astype(bf16)


def pack_kernel(
    act_ref, f_ref, g_ref, weight_ref, xlo_ref, xhi_ref, ylo_ref, yhi_ref, both_ref, w_far,
    w_ref, raw_ref, wide_ref, turn_ref, raw_sem, sem,
):
    levels, c, _ = f_ref.shape
    half = lanes_of((c, 128)) // EDGE
    raw = pltpu.make_async_copy(weight_ref, raw_ref, raw_sem)
    raw.start()
    loads = {}
    for lev in range(levels):
        for arr, ref in enumerate((f_ref, g_ref)):
            load = pltpu.make_async_copy(ref.at[lev], both_ref.at[arr, lev], sem.at[arr, lev])
            load.start()
            loads[arr, lev] = load
    raw.wait()
    spread_weight(raw_ref, w_ref, wide_ref, turn_ref)
    spread = pltpu.make_async_copy(w_ref, w_far, raw_sem)
    spread.start()
    for (arr, lev), load in loads.items():
        load.wait()
        src = both_ref.at[arr]
        live = act_ref[0, 0, lev].astype(f32).astype(bf16)
        xlo_ref[arr, lev] = src[lev, :, 0:PLANE] * live
        xhi_ref[arr, lev] = src[lev, :, 15 * PLANE : 16 * PLANE] * live
        for h in range(2):
            low = jnp.zeros((c, 128), bf16)
            high = jnp.zeros((c, 128), bf16)
            for xs in range(8):
                at = (8 * h + xs) * PLANE
                a = turned(src[lev, :, at : at + 128], EDGE * xs)
                b = turned(src[lev, :, at + 128 : at + 256], EDGE * xs + EDGE)
                low = pick(half == xs, a, low)
                high = pick(half == xs, b, high)
            ylo_ref[arr, lev, :, h * 128 : h * 128 + 128] = low * live
            yhi_ref[arr, lev, :, h * 128 : h * 128 + 128] = high * live
    spread.wait()


def near(shape, dtype):
    return pltpu.VMEM(shape, dtype)


def held(*arrays):
    return [pltpu.with_memory_space_constraint(a, pltpu.VMEM) for a in arrays]


def far_off(*arrays):
    return [pltpu.with_memory_space_constraint(a, pltpu.HBM) for a in arrays]


def pack(active, features, grads, weight, depth):
    levels, c, vox = features.shape
    apart = pl.BlockSpec(memory_space=pltpu.HBM)
    whole = pl.BlockSpec(memory_space=pltpu.VMEM)
    return pl.pallas_call(
        pack_kernel,
        in_specs=[pl.BlockSpec(memory_space=pltpu.SMEM)] + [apart] * 3,
        out_specs=[whole] * 5 + [apart],
        out_shape=[near((2, levels, c, PLANE), bf16)] * 4 + [near((2, levels, c, vox), bf16)]
        + [pltpu.HBM((2, 3 * c, depth), bf16)],
        scratch_shapes=[
            pltpu.VMEM((2, 3 * c, depth), bf16),
            pltpu.VMEM(weight.shape, bf16),
            pltpu.VMEM((c, -(-weight.shape[1] // 128) * 128), bf16),
            pltpu.VMEM((3, depth, 128), bf16),
            pltpu.SemaphoreType.DMA,
            pltpu.SemaphoreType.DMA((2, levels)),
        ],
        name="pack_faces",
        compiler_params=pltpu.CompilerParams(vmem_limit_bytes=GRANT),
    )(active, *far_off(features, grads, weight))


def turned(value, amount):
    return pltpu.roll(value, amount % 128, 1) if amount % 128 else value


def z_moved(value, mask, fill, amount):
    return pick(mask, fill, pltpu.roll(value, amount, 1))


def fill_plane(store, halves, fills, edge):
    c = halves[0].shape[0]
    lane = lanes_of((c, 128))
    z = lane % EDGE
    zero = jnp.zeros((c, 128), bf16)
    below, above = fills
    moved = (
        [z_moved(v, z == 0, f, 1) for v, f in zip(halves, below)],
        halves,
        [z_moved(v, z == EDGE - 1, f, 127) for v, f in zip(halves, above)],
    )
    if edge is None:
        rows = (zero,) * 3
    else:
        rows = (z_moved(edge, z == 0, zero, 1), edge, z_moved(edge, z == EDGE - 1, zero, 127))
    for k in range(3):
        first, last = moved[k]
        store(3 + k, 0, first)
        store(3 + k, 1, last)
        first_on, last_on = pltpu.roll(first, EDGE, 1), pltpu.roll(last, EDGE, 1)
        store(k, 0, pick(lane < EDGE, rows[k], first_on))
        store(k, 1, pick(lane < EDGE, first_on, last_on))
        first_off, last_off = (pltpu.roll(v, 128 - EDGE, 1) for v in (first, last))
        store(6 + k, 0, pick(lane >= 128 - EDGE, last_off, first_off))
        store(6 + k, 1, pick(lane >= 128 - EDGE, rows[k], last_off))


def build_inner(store, act_ref, src_ref, y_refs, arr, lev, x):
    c = src_ref.shape[1]
    other = 1 - lev
    live = act_ref[0, 0, other]
    start = x * PLANE
    halves = [src_ref[lev, :, pl.ds(start + h, 128)] for h in (0, 128)]
    turn = EDGE - 1 + lev * (128 - 2 * (EDGE - 1))
    beside = [pltpu.roll(src_ref[other, :, pl.ds(start + h, 128)], turn, 1) for h in (0, 128)]
    below_on = (live * lev).astype(f32).astype(bf16)
    above_on = (live * other).astype(f32).astype(bf16)
    below = [v * below_on for v in beside]
    above = [v * above_on for v in beside]
    edge = None
    if y_refs is not None:
        at = (x // 8) * 128
        back = EDGE * (x % 8)
        south, north = (r[arr, lev, :, at : at + 128] for r in y_refs)
        south, north = turned(south, -back), turned(north, 112 - back)
        edge = pick(lanes_of((c, 128)) < EDGE, south, north)
    fill_plane(store, halves, (below, above), edge)


def build_outer(store, plane):
    zero = jnp.zeros((plane.shape[0], 128), bf16)
    fill_plane(store, [plane[:, :128], plane[:, 128:]], ([zero] * 2,) * 2, None)


def storing(p_ref, c, start=0):
    def store(at, half, value):
        p_ref[at * c : (at + 1) * c, start + half * 128 : start + half * 128 + 128] = value

    return store


def conv_kernel(
    act_ref, src_ref, xw_far, xe_far, ys_far, yn_far, w_far, out_ref, back_ref,
    xw_ref, xe_ref, ys_ref, yn_ref, w_ref, pa_ref, pb_ref, acc_ref, res_ref, in_sem, out_sem,
):
    _, levels, c, _ = src_ref.shape
    chunks = (EDGE + 2) // CONV_CHUNK
    pairs = (
        (ys_far, ys_ref), (yn_far, yn_ref), (xw_far, xw_ref), (w_far, w_ref), (xe_far, xe_ref)
    )
    loads = [
        [
            pltpu.make_async_copy(far.at[arr], to.at[arr], in_sem.at[arr, i])
            for i, (far, to) in enumerate(pairs)
        ]
        for arr in range(2)
    ]
    for load in loads[0] + loads[1]:
        load.start()
    bufs = (pa_ref, pb_ref)
    for p_ref in bufs:
        p_ref[NEAR * c :] = jnp.zeros_like(p_ref[NEAR * c :])

    def save(arr, lev, start):
        slot = lax.rem(lev, 2)
        for i, to in enumerate((out_ref, back_ref)):

            @pl.when(arr == i)
            def _():
                copy = pltpu.make_async_copy(res_ref.at[slot], to.at[lev], out_sem.at[slot])
                copy.start() if start else copy.wait()

    def brick(item, _):
        arr, lev = item // levels, lax.rem(item, levels)
        slot = lax.rem(lev, 2)

        for i in range(2):

            @pl.when(item == i * levels)
            def _():
                for load in loads[i]:
                    load.wait()

        @pl.when(item >= 2)
        def _():
            save((item - 2) // levels, lax.rem(item - 2, levels), False)

        @pl.when(act_ref[0, 0, lev] == 0)
        def _():
            res_ref[slot] = jnp.zeros_like(res_ref[slot])

        @pl.when(act_ref[0, 0, lev] != 0)
        def _():
            def fill(p_ref, at):
                for n in range(CONV_CHUNK):
                    x = at * CONV_CHUNK + n - 1
                    store = storing(p_ref, c, n * PLANE)
                    if x < 0 or x == EDGE:
                        build_outer(store, (xw_ref if x < 0 else xe_ref)[arr, lev])
                    else:
                        build_inner(store, act_ref, src_ref.at[arr], (ys_ref, yn_ref), arr, lev, x)

            def advance(p_ref, at):
                full = jnp.dot(w_ref[arr], p_ref[...], preferred_element_type=f32)
                held = [acc_ref[0], acc_ref[1], None] if at else [None] * 3
                for n in range(CONV_CHUNK):
                    x = at * CONV_CHUNK + n - 1
                    lanes = slice(n * PLANE, (n + 1) * PLANE)
                    for dx in range(3):
                        term = full[dx * c : (dx + 1) * c, lanes]
                        i = 2 - dx
                        held[i] = term if held[i] is None else held[i] + term
                    if x > 0:
                        res_ref[slot, :, (x - 1) * PLANE : x * PLANE] = held[0].astype(bf16)
                    held = held[1:] + [None]
                acc_ref[0] = held[0]
                acc_ref[1] = held[1]

            fill(bufs[0], 0)
            for at in range(chunks):
                if at + 1 < chunks:
                    fill(bufs[(at + 1) % 2], at + 1)
                advance(bufs[at % 2], at)

        save(arr, lev, True)
        return 0

    lax.fori_loop(0, 2 * levels, brick, 0)
    for lev in range(levels - 2, levels):
        save(1, lev, False)


def conv(active, fields, faces, weights):
    _, levels, c, vox = fields.shape
    depth = weights.shape[2]
    whole = pl.BlockSpec(memory_space=pltpu.VMEM)
    apart = pl.BlockSpec(memory_space=pltpu.HBM)
    side = pltpu.VMEM((2, levels, c, PLANE), bf16)
    return pl.pallas_call(
        conv_kernel,
        in_specs=[pl.BlockSpec(memory_space=pltpu.SMEM), whole] + [apart] * 5,
        out_specs=[apart] * 2,
        out_shape=[jax.ShapeDtypeStruct((levels, c, vox), bf16)] * 2,
        scratch_shapes=[side] * 4
        + [
            pltpu.VMEM((2, 3 * c, depth), bf16),
            pltpu.VMEM((depth, CONV_CHUNK * PLANE), bf16),
            pltpu.VMEM((depth, CONV_CHUNK * PLANE), bf16),
            pltpu.VMEM((2, c, PLANE), f32),
            pltpu.VMEM((2, c, vox), bf16),
            pltpu.SemaphoreType.DMA((2, 5)),
            pltpu.SemaphoreType.DMA((2,)),
        ],
        name="conv",
        compiler_params=pltpu.CompilerParams(vmem_limit_bytes=GRANT),
    )(active, *held(fields), *far_off(*faces, weights))


def wgrad_kernel(act_ref, both_ref, out_ref, pa_ref, pb_ref, g_ref):
    src_ref, grad_ref = both_ref.at[0], both_ref.at[1]
    c = src_ref.shape[1]
    chunks = EDGE // CHUNK
    wide = CHUNK * PLANE
    out_ref[...] = jnp.zeros_like(out_ref)
    bufs = (pa_ref, pb_ref)
    for p_ref in bufs:
        p_ref[NEAR * c :] = jnp.zeros_like(p_ref[NEAR * c :])
    g_ref[:, :PLANE] = jnp.zeros((c, PLANE), bf16)
    g_ref[:, (EDGE + 1) * PLANE :] = jnp.zeros((c, PLANE), bf16)

    def level(lev, _):
        @pl.when(act_ref[0, 0, lev] != 0)
        def _():
            g_ref[:, PLANE : (EDGE + 1) * PLANE] = grad_ref[lev]

            def fill(p_ref, at):
                for n in range(CHUNK):
                    store = storing(p_ref, c, n * PLANE)
                    build_inner(store, act_ref, src_ref, None, 0, lev, at * CHUNK + n)

            def gather(p_ref, at):
                starts = [(at * CHUNK + 2 - dx) * PLANE for dx in range(3)]
                out_ref[...] += lax.dot_general(
                    jnp.concatenate([g_ref[:, i : i + wide] for i in starts], axis=0),
                    p_ref[...],
                    (((1,), (1,)), ((), ())),
                    preferred_element_type=f32,
                )

            fill(bufs[0], 0)
            for at in range(chunks):
                if at + 1 < chunks:
                    fill(bufs[(at + 1) % 2], at + 1)
                gather(bufs[at % 2], at)

        return 0

    lax.fori_loop(0, 2, level, 0)


def wgrad(active, fields, depth):
    c = fields.shape[2]
    whole = pl.BlockSpec(memory_space=pltpu.VMEM)
    return pl.pallas_call(
        wgrad_kernel,
        in_specs=[pl.BlockSpec(memory_space=pltpu.SMEM), whole],
        out_specs=whole,
        out_shape=near((3 * c, depth), f32),
        scratch_shapes=[
            pltpu.VMEM((depth, CHUNK * PLANE), bf16),
            pltpu.VMEM((depth, CHUNK * PLANE), bf16),
            pltpu.VMEM((c, (EDGE + 2) * PLANE), bf16),
        ],
        name="wgrad",
        compiler_params=pltpu.CompilerParams(vmem_limit_bytes=GRANT),
    )(active, *held(fields))


def rim_kernel(
    sum_ref, gxl_ref, gxh_ref, gyl_ref, gyh_ref, xw_ref, xe_ref, ys_ref, yn_ref,
    out_far, px_ref, py_ref, row_ref, out_ref, sem,
):
    c = gxl_ref.shape[2]
    levels = gxl_ref.shape[1]
    px_ref[:, NEAR * c :] = jnp.zeros_like(px_ref[:, NEAR * c :])
    py_ref[...] = jnp.zeros_like(py_ref)

    def both(ref):
        return jnp.concatenate([ref[1, k] for k in range(levels)], axis=1)

    def gathered(left, right):
        return lax.dot_general(left, right, (((1,), (1,)), ((), ())), preferred_element_type=f32)

    for side, halo in enumerate((xw_ref, xe_ref)):
        for k in range(levels):
            build_outer(storing(px_ref.at[side], c, k * PLANE), halo[0, k])
    for side, halo in enumerate((ys_ref, yn_ref)):
        for k in range(levels):

            def store(at, half, value):
                row = 64 * side + (at % 3) * c
                col = k * PLANE + half * 128
                py_ref[side, at // 3, row : row + c, col : col + 128] = value

            build_outer(store, halo[0, k])
    split = py_ref.shape[2]
    depth = sum_ref.shape[1]
    far = depth - split
    end = jnp.zeros((c, 128), f32)
    kept = None
    for dx in range(3):
        total = sum_ref[dx * c : (dx + 1) * c]
        if dx != 1:
            own = gxl_ref if dx == 0 else gxh_ref
            total = total + gathered(both(own), px_ref[dx // 2])
        low = total[:, :split] + gathered(both(gyl_ref), py_ref[0, dx])
        high = total[:, far:] + gathered(both(gyh_ref), py_ref[1, dx])
        total = jnp.concatenate([low, total[:, split:far], high], axis=1)
        start = dx * NEAR * c
        tile = start // 128 * 128
        if dx:
            total = pltpu.roll(jnp.concatenate([total, end], axis=1), start - tile, 1)
            row_ref[tile // 128] = kept + total[:, :128]
            total = total[:, 128:]
            tile += 128
        size = total.shape[1]
        if dx < 2:
            size -= 128
            kept = total[:, size:]
        for i in range(size // 128):
            row_ref[tile // 128 + i] = total[:, i * 128 : i * 128 + 128]
    scatter_rows(row_ref, out_ref, out_far, sem)


def scatter_rows(row_ref, out_ref, out_far, sem):
    tiles, count, _ = row_ref.shape
    groups = count // 3
    length = 3 * NEAR * count
    share = 3 * length // 4
    room = out_ref.shape[2] * 128
    lane = lanes_of((groups, 128))
    copies = []
    rows = [
        jnp.concatenate([row_ref.at[t][pl.ds(r, groups, stride=3), :] for t in range(tiles)], axis=1)
        for r in range(3)
    ]
    for q in range(4):
        first = q * share
        r, start = first // length, first % length
        tile = start // 128 * 128
        value = rows[r][:, tile : tile + room]
        if start - tile:
            value = pltpu.roll(value, value.shape[1] - (start - tile), 1)
        left = length - start
        if left < share:
            seam = left // 128 * 128
            after = rows[r + 1][:, : room - seam]
            after = pltpu.roll(after, left - seam, 1)
            middle = pick(lane < left - seam, value[:, seam : seam + 128], after[:, :128])
            value = jnp.concatenate([value[:, :seam], middle, after[:, 128:]], axis=1)
        out_ref[q] = value.reshape(groups, room // 128, 128)
        copies.append(pltpu.make_async_copy(out_ref.at[q], out_far.at[:, q], sem.at[q]))
        copies[-1].start()
    for copy in copies:
        copy.wait()


def rim(sums, own, halos, rows):
    levels, c = own[0].shape[1:3]
    depth = sums.shape[1]
    whole = pl.BlockSpec(memory_space=pltpu.VMEM)
    return pl.pallas_call(
        rim_kernel,
        in_specs=[whole] * 9,
        out_specs=pl.BlockSpec(memory_space=pltpu.HBM),
        out_shape=pltpu.HBM((c // 3, 4, rows, 128), f32),
        scratch_shapes=[
            pltpu.VMEM((2, depth, levels * PLANE), bf16),
            pltpu.VMEM((2, 3, 384, levels * PLANE), bf16),
            pltpu.VMEM((-(-3 * NEAR * c // 128), c, 128), f32),
            pltpu.VMEM((4, c // 3, rows, 128), f32),
            pltpu.SemaphoreType.DMA((4,)),
        ],
        name="rim",
        compiler_params=pltpu.CompilerParams(vmem_limit_bytes=GRANT),
    )(*held(sums, *own, *halos))


def neighbours(low, high, axis):
    count = lax.axis_size(axis)
    forward = [(i, i + 1) for i in range(count - 1)]
    backward = [(j, i) for i, j in forward]
    return lax.ppermute(high, axis, forward), lax.ppermute(low, axis, backward)


def body(features, grad_out, weight, active):
    levels, c, vox = features.shape[2:]
    active, = far_off(active)
    depth = -(-NEAR * c // 128) * 128
    fields = features.reshape(levels, c, vox)
    grads = grad_out.reshape(levels, c, vox)
    *own, cells, weights = pack(active, fields, grads, weight, depth)
    halos = neighbours(own[0], own[1], "gx") + neighbours(own[2], own[3], "gy")

    unit = 3 * 3 * NEAR * c // 4
    rows = -(-unit // 1024) * 8
    shares = rim(wgrad(active, cells, depth), own, halos, rows).reshape(-1, rows, 128)
    parts = lax.axis_size("gx") * lax.axis_size("gy")
    share = weight.size // parts
    if parts != shares.shape[0]:
        shares = shares.reshape(-1, rows * 128)[:, :unit].reshape(parts, share)
        shares = jnp.pad(shares, ((0, 0), (0, -share % 1024))).reshape(parts, -1, 128)
    swapped = lax.all_to_all(shares, ("gx", "gy"), 0, 0, tiled=True)
    norm_scale = 1.0 / math.sqrt(parts * levels * vox)
    summed = swapped.sum(0).reshape(-1)[:share] * norm_scale

    out, grad_in = conv(active, cells, halos, weights)
    return out[None, None], grad_in[None, None], summed


def solution(mesh):
    placed = (
        P("gx", "gy", None, None, None),
        P("gx", "gy", None, None, None),
        P(),
        P("gx", "gy", None),
    )
    return jax.shard_map(
        body,
        mesh=mesh,
        in_specs=placed,
        out_specs=(
            P("gx", "gy", None, None, None),
            P("gx", "gy", None, None, None),
            P(("gx", "gy")),
        ),
        check_vma=False,
    )
```
